32 devices in a mesh: gx: 8 (over z, y), gy: 4 (over x, core).
Axes of the slice: x: 2, y: 2, z: 4, core: 2. Of those that a mesh axis runs over, the one named last changes fastest.
Arguments:
- fields: float32 [6, 128, 96, 128], P(None, 'gx', 'gy'), may hold values from -6 to 6
- material: int32 [128, 96, 128], P('gx', 'gy'), may hold values from 0 to 15
- permittivity: float32 [16], replicated, may hold values from 1 to 4
- patch_cell: int32 [8192], P(('gx', 'gy')), may hold values from 0 to 49151
- patch_owner: int32 [8192, 1], P(('gx', 'gy')), may hold values from 0 to 31; in each aligned block of 256 rows (0 to 255, 256 to 511, ...) at most 16 rows name the same one
Outputs:
- new_fields: float32 [6, 128, 96, 128], P(None, 'gx', 'gy')
- far_field: float32 [12, 4096], P(None, ('gx', 'gy'))
The draws below stay inside these ranges and needn't reach their ends.
Inputs may be any that keep to these rules, and one draw needn't show every extreme that they name: `patch_cell`: an index into the cells of the patch's own device block, x slowest and z fastest. `patch_owner`: among the rows of one device no sector is named by more than 16 rows, a bound that some block reaches; every sector is named by some row.
All inputs are finite; a program needn't handle non-finite values.
Results may differ from the reference program's by a relative error of at most 0.00022.
Values sent between devices are 32-bit elements; how exact they have to be, the bound alone decides.
A program may use at most 128 MiB of HBM per device.

```python
import math
import jax
import jax.numpy as jnp
import numpy as np
from jax import lax

CX = 16
CY = 24
NZ = 128
P_DEV = 256
ANG_DEV = 128
COURANT = 64
MATERIALS = 16
NX = 128
NY = 96
OWNERS = 32
PATCHES = 8192
CAP = 16
N_GX = 8
N_GY = 4


def plant(drawn, stream_key, least, top_value):
    shape = drawn.shape
    index_at = [jax.random.randint(jax.random.fold_in(stream_key, axis), (), 0, shape[axis]) for axis in range(len(shape))]
    drawn = drawn.at[tuple(index_at)].set(least)
    longest = shape.index(max(shape))
    index_at[longest] = (index_at[longest] + 1) % shape[longest]
    return drawn.at[tuple(index_at)].set(top_value)


def steps_of(rng, dims, cuts, smallest, largest):
    level, own = 1.0, jax.random.fold_in(rng, 6)
    for dim, shards_of in cuts:
        heights = jnp.exp(jax.random.uniform(jax.random.fold_in(own, dim), (shards_of,), jnp.float32, smallest / len(cuts), largest / len(cuts)))
        level = level * jnp.repeat(heights, dims[dim] // shards_of).reshape([-1 if axis == dim else 1 for axis in range(len(dims))])
    return level


def deal_out(stream_key, own, number, rows, count, top, most, skew):
    sequence = jax.random.permutation(stream_key, count)
    packed, usual = portions_of(count, rows * top, most, skew, True), portions_of(count, rows * top, most, skew, False)
    places = jnp.arange(count)

    def named(lengths, turn):
        used = int((lengths > 0).sum())
        fixed = max(1, used // 4)
        passed = fixed + (places - fixed + turn * (used - fixed)) % max(1, count - fixed)
        return jnp.zeros((count,), jnp.int32).at[sequence[jnp.where(places < fixed, places, passed)]].set(jnp.asarray(lengths, jnp.int32))

    lengths = jnp.where(number % 4 == 0, named(packed, number // 4), named(usual, number - number // 4 - 1))
    mixed = jax.random.permutation(jax.random.fold_in(own, 3), count)
    giver, taker = mixed[0:count // 2 * 2:2], mixed[1:count // 2 * 2:2]
    room = jnp.minimum(lengths[giver] - 1, most - lengths[taker]) // 2
    room = jnp.where((giver == sequence[0]) | (taker == sequence[0]) | (lengths[taker] == 0), 0, jnp.maximum(room, 0))
    passed = jax.random.randint(jax.random.fold_in(own, 4), (count // 2,), 0, 1 << 20) % (room + 1)
    lengths = lengths.at[giver].add(-passed).at[taker].add(passed)
    labels = jnp.searchsorted(jnp.cumsum(lengths), jnp.arange(rows * top), side="right").astype(jnp.int32)
    grid = labels.reshape(top, rows).T
    grid = grid[jax.random.permutation(jax.random.fold_in(own, 1), rows)]
    turn = jax.random.randint(jax.random.fold_in(own, 2), (rows, 1), 0, top)
    return jnp.take_along_axis(grid, (jnp.arange(top)[None, :] + turn) % top, axis=1)


def portions_of(count, total, bound, skew, full):
    loads = [(1 << 20) // math.isqrt(rank ** skew) + 1 for rank in range(1, count + 1)]
    largest = bound if full else min(bound, max(-(-total // count), total * loads[0] // sum(loads)))
    least = 1 if total - largest >= count - 1 else 0
    given, spare = [largest] + [least] * (count - 1), total - largest - least * (count - 1)
    while spare > 0:
        movable = [i for i in range(1, count) if given[i] < largest] or [i for i in range(1, count) if given[i] < bound]
        mass, remaining = sum([loads[i] for i in movable]), spare
        for i in movable:
            more = min(bound - given[i], max(1, remaining * loads[i] // mass), spare)
            given[i] = given[i] + more
            spare = spare - more
    return np.array(given)


def bell_draw(stream_key, shape, deviation, limit, shards=(), held_as=jnp.bfloat16):
    result = jax.random.normal(stream_key, shape, jnp.float32) * deviation
    if len(shards) > 0:
        result = steps_of(stream_key, shape, shards, -0.22, 0.18) * result
    return jnp.clip(result, min=-limit, max=limit).astype(held_as)


def setup_inputs(seed: int = 0) -> dict:
    streams_of = jax.random.split(jax.random.key(seed), 6)
    fields = bell_draw(streams_of[0], (6, NX, NY, NZ), 1.0, 6.0, ((1, 8), (2, 4)), jnp.float32)
    material = plant(jax.random.randint(streams_of[1], (NX, NY, NZ), 0, MATERIALS), jax.random.fold_in(streams_of[1], 1), 0, MATERIALS - 1).astype(jnp.int32)
    permittivity = jnp.clip(jnp.exp(jax.random.uniform(streams_of[2], (MATERIALS,), jnp.float32, math.log(1.0), math.log(4.0))), 1.0, 4.0)
    patch_cell = plant(jax.random.randint(streams_of[3], (PATCHES,), 0, CX * CY * NZ), jax.random.fold_in(streams_of[3], 1), 0, (CX * CY * NZ) - 1).astype(jnp.int32)
    patch_owner_keys = jax.random.split(jax.random.fold_in(streams_of[4], 1), PATCHES // P_DEV)
    patch_owner_turns = jax.random.permutation(jax.random.fold_in(streams_of[4], 3), PATCHES // P_DEV)
    patch_owner = jax.vmap(lambda own, number: deal_out(jax.random.fold_in(streams_of[4], 2), own, number, P_DEV, OWNERS, 1, CAP, 2))(patch_owner_keys, patch_owner_turns).reshape((PATCHES, 1))
    return dict(fields=fields, material=material, permittivity=permittivity, patch_cell=patch_cell, patch_owner=patch_owner)


KAPPA = 0.5

def explicit(padded, curl_coef, half_step):
    centre = padded[:, 1:-1, 1:-1]

    def slope_x(member):
        return 0.5 * (padded[member, 2:, 1:-1] - padded[member, :-2, 1:-1])

    def slope_y(member):
        return 0.5 * (padded[member, 1:-1, 2:] - padded[member, 1:-1, :-2])

    def slope_z(member):
        ground = jnp.pad(centre[member], ((0, 0), (0, 0), (1, 1)))
        return 0.5 * (ground[:, :, 2:] - ground[:, :, :-2])
    curl_h = [slope_y(5) - slope_z(4), slope_z(3) - slope_x(5), slope_x(4) - slope_y(3)]
    curl_e = [slope_y(2) - slope_z(1), slope_z(0) - slope_x(2), slope_x(1) - slope_y(0)]
    electric = [centre[member] + curl_coef * curl_h[member] for member in range(3)]
    magnetic = [centre[3 + member] - half_step * curl_e[member] for member in range(3)]
    return jnp.stack(electric + magnetic)

def factor_lines(coef_lines):

    def advance(upper_prev, coef_row):
        pivot = 1.0 / (1.0 + 2.0 * coef_row + coef_row * upper_prev)
        upper_now = -coef_row * pivot
        return (upper_now, (upper_now, pivot))
    ignored, (uppers, pivots) = lax.scan(advance, jnp.zeros_like(coef_lines[0]), coef_lines)
    return (uppers, pivots)

def sweep_lines(coef_lines, uppers, pivots, right_lines):

    def forward(carry_prev, rows):
        coef_row, pivot, right_row = rows
        now_value = (right_row + coef_row * carry_prev) * pivot
        return (now_value, now_value)
    start_zero = jnp.zeros_like(right_lines[0] * coef_lines[0])
    ignored, reduced = lax.scan(forward, start_zero, (coef_lines, pivots, right_lines))

    def backward(next_value, rows):
        upper_row, reduced_row = rows
        now_value = reduced_row - upper_row * next_value
        return (now_value, now_value)
    ignored, solved = lax.scan(backward, start_zero, (uppers, reduced), reverse=True)
    return solved

def solve_leading(stack, coef_lines):
    uppers, pivots = factor_lines(coef_lines)

    def one_component(component):
        return sweep_lines(coef_lines, uppers, pivots, component)
    return lax.map(one_component, stack)

def far_phase(pos_x, pos_y, pos_z, owner_f, owners, angle_count):
    theta = math.pi * (jnp.arange(angle_count, dtype=jnp.float32) + 0.5) / angle_count
    azimuth = owner_f * (2.0 * math.pi / owners)
    sin_theta = jnp.sin(theta)[None, :]
    cos_theta = jnp.cos(theta)[None, :]
    cos_phi = jnp.cos(azimuth)[:, None]
    sin_phi = jnp.sin(azimuth)[:, None]
    return KAPPA * (pos_x[:, None] * sin_theta * cos_phi + pos_y[:, None] * sin_theta * sin_phi + pos_z[:, None] * cos_theta)

def reference(fields, material, permittivity, patch_cell, patch_owner):
    eps = permittivity[material]
    half_step = COURANT / 2.0
    implicit_coef = half_step * half_step / eps
    curl_coef = half_step / eps
    padded = jnp.pad(fields, ((0, 0), (1, 1), (1, 1), (0, 0)))
    first_side = explicit(padded, curl_coef, half_step)
    mid_fields = solve_leading(first_side, implicit_coef)
    padded = jnp.pad(mid_fields, ((0, 0), (1, 1), (1, 1), (0, 0)))
    second_side = explicit(padded, curl_coef, half_step)
    moved = jnp.moveaxis(second_side, 2, 1)
    coef_y = jnp.transpose(implicit_coef, (1, 0, 2))
    new_fields = jnp.moveaxis(solve_leading(moved, coef_y), 1, 2)
    owners = N_GX * N_GY
    device = jnp.arange(PATCHES, dtype=jnp.int32) // P_DEV
    block_x = device // N_GY
    block_y = device % N_GY
    grid_x = block_x * CX + patch_cell // (CY * NZ)
    grid_y = block_y * CY + patch_cell // NZ % CY
    grid_z = patch_cell % NZ
    samples = new_fields[:, grid_x, grid_y, grid_z]
    owner = patch_owner[:, 0]
    phases = far_phase(grid_x.astype(jnp.float32), grid_y.astype(jnp.float32), grid_z.astype(jnp.float32), owner.astype(jnp.float32), owners, ANG_DEV)
    cosine = jnp.cos(phases)
    sine = jnp.sin(phases)
    values_t = jnp.transpose(samples)
    terms = jnp.concatenate([values_t[:, :, None] * cosine[:, None, :], values_t[:, :, None] * sine[:, None, :]], axis=1)
    summed = jax.ops.segment_sum(terms, owner, num_segments=owners)
    far_field = jnp.transpose(summed, (1, 0, 2)).reshape(12, owners * ANG_DEV) * (1.0 / math.sqrt(P_DEV))
    return (new_fields, far_field)
```

```python
import functools
import math

import jax
import jax.numpy as jnp
from jax import lax
from jax.experimental import pallas as pl
from jax.experimental.pallas import tpu as pltpu
from jax.sharding import PartitionSpec as P

ANG_DEV = 128
COURANT = 64
KAPPA = 0.5
MESH = pl.DeviceIdType.MESH
Y_MEMBERS = (0, 2, 3, 5)
CHUNKS = ((0, 2), (2, 2), (4, 2))


def slope_rows(value, low_row, high_row):
    rows = value.shape[0]
    at = lax.broadcasted_iota(jnp.int32, value.shape, 0)
    below = jnp.where(at == 0, low_row, pltpu.roll(value, 1, 0))
    above = jnp.where(at == rows - 1, high_row, pltpu.roll(value, rows - 1, 0))
    return 0.5 * (above - below)


def slope_lanes(value):
    lanes = value.shape[1]
    at = lax.broadcasted_iota(jnp.int32, value.shape, 1)
    below = jnp.where(at == 0, 0.0, pltpu.roll(value, 1, 1))
    above = jnp.where(at == lanes - 1, 0.0, pltpu.roll(value, lanes - 1, 1))
    return 0.5 * (above - below)


def updated(centre, slope_x, slope_y, curl_coef, half_step):
    slope_z = lambda member: slope_lanes(centre[member])
    curl_h = [slope_y(5) - slope_z(4), slope_z(3) - slope_x(5), slope_x(4) - slope_y(3)]
    curl_e = [slope_y(2) - slope_z(1), slope_z(0) - slope_x(2), slope_x(1) - slope_y(0)]
    return [centre[m] + curl_coef * curl_h[m] for m in range(3)] + [
        centre[3 + m] - half_step * curl_e[m] for m in range(3)
    ]


def factor(length, coef_at, gain_ref, pivot_ref, left_ref, right_ref):
    zero = jnp.zeros(gain_ref.shape[1:], jnp.float32)

    def forward(i, carry):
        gain_prev, left_prev = carry
        coef = coef_at(i)
        pivot = 1.0 / (1.0 + 2.0 * coef - coef * gain_prev)
        gain = coef * pivot
        left = gain * left_prev
        gain_ref[i] = gain
        pivot_ref[i] = pivot
        left_ref[i] = left
        return gain, left

    lax.fori_loop(0, length, forward, (zero, jnp.ones_like(zero)))

    def backward(k, carry):
        left_next, right_next = carry
        i = length - 1 - k
        gain = gain_ref[i]
        left = left_ref[i] + gain * left_next
        right = gain * right_next
        left_ref[i] = left
        right_ref[i] = right
        return left, right

    lax.fori_loop(0, length, backward, (zero, jnp.ones_like(zero)))


def sweep_back(length, gain_ref, solved_ref):
    def backward(k, carry):
        i = length - 1 - k
        gain = gain_ref[i]
        now = [solved_ref[m, i] + gain * carry[m] for m in range(6)]
        for m in range(6):
            solved_ref[m, i] = now[m]
        return tuple(now)

    zero = jnp.zeros(gain_ref.shape[1:], jnp.float32)
    lax.fori_loop(0, length, backward, (zero,) * 6)


class Line:
    def __init__(self, axis, count, refs):
        (self.mat_out, self.mat_in, self.rhs_out, self.rhs_in, self.plan, self.gains, self.ends,
         self.mat_sems, self.rhs_sems) = refs
        self.axis = axis
        self.count = count
        self.steps = count.bit_length() - 1
        self.me = lax.axis_index(axis)

    def near(self, k):
        return 1 - (self.me // 2**k) % 2

    def partner(self, k):
        return {self.axis: self.me + (2 * self.near(k) - 1) * 2**k}

    def mat_copy(self, k):
        return pltpu.make_async_remote_copy(
            self.mat_out.at[k], self.mat_in.at[k], self.mat_sems.at[0, k], self.mat_sems.at[1, k],
            device_id=self.partner(k), device_id_type=MESH)

    def rhs_copy(self, k, j):
        first, size = CHUNKS[j]
        if k == self.steps - 1:
            source = self.rhs_out.at[k, self.near(k), pl.ds(first, size)]
            target = self.rhs_in.at[k, 0, pl.ds(first, size)]
        else:
            source = self.rhs_out.at[k, :, pl.ds(first, size)]
            target = self.rhs_in.at[k, :, pl.ds(first, size)]
        return pltpu.make_async_remote_copy(
            source, target, self.rhs_sems.at[0, k, j], self.rhs_sems.at[1, k, j],
            device_id=self.partner(k), device_id_type=MESH)

    def mat_start(self, left_ref, right_ref):
        last = left_ref.shape[0] - 1
        for end, at in ((0, 0), (1, last)):
            self.mat_out[0, 2 * end] = left_ref[at]
            self.mat_out[0, 2 * end + 1] = right_ref[at]
        one, zero = jnp.ones(left_ref.shape[1:], jnp.float32), jnp.zeros(left_ref.shape[1:], jnp.float32)
        self.gains[0] = one
        self.gains[1] = zero
        self.gains[2] = zero
        self.gains[3] = one
        self.mat_copy(0).start()

    def mat_merge(self, k):
        self.mat_copy(k).wait_recv()
        n = self.near(k)
        f = 1 - n
        mine = lambda end, side: self.mat_out[k, 2 * end + side]
        other = lambda end, side: self.mat_in[k, 2 * end + side]
        m_nn, m_fn, m_nf, m_ff = mine(n, n), mine(f, n), mine(n, f), mine(f, f)
        o_nn, o_fn, o_nf, o_ff = other(f, f), other(n, f), other(f, n), other(n, n)
        inv = 1.0 / (1.0 - m_nn * o_nn)
        o_by_m = o_nn * m_nf * inv
        o_by_o = o_nf * inv
        m_by_m = m_nf * inv
        m_by_o = m_nn * o_nf * inv
        gain_in, gain_out = self.gains[n], self.gains[2 + n]
        for slot, value in enumerate((inv, o_nn * inv, m_nn * inv, m_fn, o_fn, gain_in, gain_out)):
            self.plan[k, slot] = value
        if k < self.steps - 1:
            self.mat_out[k + 1, 2 * f + f] = m_ff + m_fn * o_by_m
            self.mat_out[k + 1, 2 * f + n] = m_fn * o_by_o
            self.mat_out[k + 1, 2 * n + n] = o_ff + o_fn * m_by_o
            self.mat_out[k + 1, 2 * n + f] = o_fn * m_by_m
            self.mat_copy(k + 1).start()
            self.gains[f] = self.gains[f] + gain_in * o_by_m
            self.gains[2 + f] = self.gains[2 + f] + gain_out * o_by_m
            self.gains[n] = gain_in * o_by_o
            self.gains[2 + n] = gain_out * o_by_o

    def rhs_start(self, solved_ref):
        last = solved_ref.shape[1] - 1
        for j, (first, size) in enumerate(CHUNKS):
            for m in range(first, first + size):
                self.rhs_out[0, 0, m] = solved_ref[m, 0]
                self.rhs_out[0, 1, m] = solved_ref[m, last]
            self.rhs_copy(0, j).start()

    def rhs_merge(self, k, j):
        first, size = CHUNKS[j]
        self.rhs_copy(k, j).wait_recv()
        n = self.near(k)
        f = 1 - n
        ending = k == self.steps - 1
        inv, o_nn, m_nn, m_fn, o_fn, gain_in, gain_out = [self.plan[k, slot] for slot in range(7)]
        for m in range(first, first + size):
            mine = self.rhs_out[k, n, m]
            other = self.rhs_in[k, 0, m] if ending else self.rhs_in[k, f, m]
            o_value = other * inv + o_nn * mine
            if not ending:
                m_value = mine * inv + m_nn * other
                self.rhs_out[k + 1, f, m] = self.rhs_out[k, f, m] + m_fn * o_value
                self.rhs_out[k + 1, n, m] = self.rhs_in[k, n, m] + o_fn * m_value
            into, out_of = gain_in * o_value, gain_out * o_value
            if k > 0:
                into, out_of = self.ends[0, m] + into, self.ends[1, m] + out_of
            self.ends[0, m] = into
            self.ends[1, m] = out_of
        if not ending:
            self.rhs_copy(k + 1, j).start()

    def drain(self):
        for k in range(self.steps):
            self.mat_copy(k).wait_send()
            for j in range(len(CHUNKS)):
                self.rhs_copy(k, j).wait_send()


def both_ways(axis, count, out_low, out_high, in_low, in_high, sems):
    me = lax.axis_index(axis)
    up = lambda: pltpu.make_async_remote_copy(
        out_high, in_low, sems.at[0], sems.at[1], device_id={axis: me + 1}, device_id_type=MESH)
    down = lambda: pltpu.make_async_remote_copy(
        out_low, in_high, sems.at[2], sems.at[3], device_id={axis: me - 1}, device_id_type=MESH)

    def start():
        @pl.when(me < count - 1)
        def _():
            up().start()

        @pl.when(me > 0)
        def _():
            down().start()

        @pl.when(me == 0)
        def _():
            in_low[...] = jnp.zeros(in_low.shape, jnp.float32)

        @pl.when(me == count - 1)
        def _():
            in_high[...] = jnp.zeros(in_high.shape, jnp.float32)

    def wait():
        @pl.when(me > 0)
        def _():
            up().wait_recv()

        @pl.when(me < count - 1)
        def _():
            down().wait_recv()

    def drain():
        @pl.when(me < count - 1)
        def _():
            up().wait_send()

        @pl.when(me > 0)
        def _():
            down().wait_send()

    return start, wait, drain


def greet(axis, count, barrier):
    me = lax.axis_index(axis)

    @pl.when(me > 0)
    def _():
        pl.semaphore_signal(barrier, inc=1, device_id={axis: me - 1}, device_id_type=MESH)

    @pl.when(me < count - 1)
    def _():
        pl.semaphore_signal(barrier, inc=1, device_id={axis: me + 1}, device_id_type=MESH)

    steps = count.bit_length() - 1
    for k in range(1, steps):
        side = 1 - 2 * ((me // 2**k) % 2)
        pl.semaphore_signal(barrier, inc=1, device_id={axis: me + side * 2**k}, device_id_type=MESH)
    inner = jnp.where(me > 0, 1, 0) + jnp.where(me < count - 1, 1, 0)
    return inner + steps - 1


def step_kernel(nx, ny, cx, cy, cz, fields_hbm, material_ref, permit_ref, out_ref,
                grid_x, grid_y, y_out, y_low, y_high, coef_x,
                gain_x, pivot_x, left_x, right_x, solved_x,
                coef_y, gain_y, pivot_y, left_y, right_y, solved_y,
                load_sem, halo_sems, *line_refs):
    half_step = COURANT / 2.0
    barrier = pltpu.get_barrier_semaphore()
    load = pltpu.make_async_copy(fields_hbm, grid_x.at[:, pl.ds(1, cx)], load_sem)
    load.start()
    waits = greet("gx", nx, barrier) + greet("gy", ny, barrier)
    line_x = Line("gx", nx, line_refs[:9])
    line_y = Line("gy", ny, line_refs[9:])

    x_halo = both_ways("gx", nx, grid_x.at[pl.ds(1, 5), 1], grid_x.at[pl.ds(1, 5), cx],
                       grid_x.at[pl.ds(1, 5), 0], grid_x.at[pl.ds(1, 5), cx + 1], halo_sems.at[0])
    y_halo = both_ways("gy", ny, y_out.at[0], y_out.at[1], y_low, y_high, halo_sems.at[1])
    mid_halo = both_ways("gy", ny, grid_y.at[:, pl.ds(cx, cx)], grid_y.at[:, pl.ds(cx * cy, cx)],
                         grid_y.at[:, pl.ds(0, cx)], grid_y.at[:, pl.ds(cx * (cy + 1), cx)],
                         halo_sems.at[2])
    load.wait()
    for slot, member in enumerate(Y_MEMBERS):
        y_out[0, slot] = jnp.concatenate([grid_x[member, 1 + i, 0:1] for i in range(cx)], axis=0)
        y_out[1, slot] = jnp.concatenate([grid_x[member, 1 + i, cy - 1:cy] for i in range(cx)], axis=0)
    pl.semaphore_wait(barrier, waits)
    x_halo[0]()
    y_halo[0]()

    def coefs(i, carry):
        which = material_ref[i]
        permit = jnp.zeros(which.shape, jnp.float32)
        for entry in range(permit_ref.shape[0]):
            permit = jnp.where(which == entry, permit_ref[entry], permit)
        coef_x[pl.ds(pl.multiple_of(i * cy, 8), cy), :] = (half_step * half_step) / permit
        return carry

    lax.fori_loop(0, cx, coefs, 0)
    coef_plane = lambda i: coef_x[pl.ds(pl.multiple_of(i * cy, 8), cy), :]
    factor(cx, coef_plane, gain_x, pivot_x, left_x, right_x)
    line_x.mat_start(left_x, right_x)

    for j in range(cy):
        coef_y[j] = coef_x[pl.ds(j, cx, stride=cy), :]
    factor(cy, lambda j: coef_y[j], gain_y, pivot_y, left_y, right_y)
    line_y.mat_start(left_y, right_y)

    x_halo[1]()
    y_halo[1]()
    y_slot = {member: slot for slot, member in enumerate(Y_MEMBERS)}

    def forward_x(i, carry):
        centre = [grid_x[m, i + 1] for m in range(6)]
        slope_x = lambda m: 0.5 * (grid_x[m, i + 2] - grid_x[m, i])
        slope_y = lambda m: slope_rows(
            centre[m], y_low[y_slot[m], pl.ds(i, 1), :], y_high[y_slot[m], pl.ds(i, 1), :])
        right = updated(centre, slope_x, slope_y, coef_plane(i) * (1.0 / half_step), half_step)
        gain, pivot = gain_x[i], pivot_x[i]
        now = [right[m] * pivot + gain * carry[m] for m in range(6)]
        for m in range(6):
            solved_x[m, i] = now[m]
        return tuple(now)

    lax.fori_loop(0, cx, forward_x, (jnp.zeros((cy, cz), jnp.float32),) * 6)
    sweep_back(cx, gain_x, solved_x)
    line_x.rhs_start(solved_x)
    for k in range(max(line_x.steps, line_y.steps)):
        if k < line_x.steps:
            line_x.mat_merge(k)
        if k < line_y.steps:
            line_y.mat_merge(k)
    for k in range(line_x.steps):
        for j in range(len(CHUNKS)):
            line_x.rhs_merge(k, j)

    for i in range(cx):
        left, right = left_x[i], right_x[i]
        for m in range(6):
            grid_y[m, pl.ds(cx + i, cy, stride=cx), :] = (
                solved_x[m, i] + left * line_x.ends[0, m] + right * line_x.ends[1, m])
    mid_halo[0]()
    mid_halo[1]()

    y_plane = lambda m, j: grid_y[m, pl.ds(pl.multiple_of(j * cx, 8), cx), :]

    def forward_y(j, carry):
        centre = [y_plane(m, j + 1) for m in range(6)]
        slope_y = lambda m: 0.5 * (y_plane(m, j + 2) - y_plane(m, j))
        slope_x = lambda m: slope_rows(
            centre[m], line_x.ends[0, m, pl.ds(j, 1), :], line_x.ends[1, m, pl.ds(j, 1), :])
        right = updated(centre, slope_x, slope_y, coef_y[j] * (1.0 / half_step), half_step)
        gain, pivot = gain_y[j], pivot_y[j]
        now = [right[m] * pivot + gain * carry[m] for m in range(6)]
        for m in range(6):
            solved_y[m, j] = now[m]
        return tuple(now)

    lax.fori_loop(0, cy, forward_y, (jnp.zeros((cx, cz), jnp.float32),) * 6)
    sweep_back(cy, gain_y, solved_y)
    line_y.rhs_start(solved_y)
    for k in range(line_y.steps):
        for j in range(len(CHUNKS)):
            line_y.rhs_merge(k, j)
    for j in range(cy):
        left, right = left_y[j], right_y[j]
        for m in range(6):
            out_ref[m, pl.ds(j, cx, stride=cy), :] = (
                solved_y[m, j] + left * line_y.ends[0, m] + right * line_y.ends[1, m])
    for halo in (x_halo, y_halo, mid_halo):
        halo[2]()
    line_x.drain()
    line_y.drain()


def line_scratch(count, rows, lanes):
    steps = count.bit_length() - 1
    f32 = jnp.float32
    return [
        pltpu.VMEM((steps, 4, rows, lanes), f32),
        pltpu.VMEM((steps, 4, rows, lanes), f32),
        pltpu.VMEM((steps, 2, 6, rows, lanes), f32),
        pltpu.VMEM((steps, 2, 6, rows, lanes), f32),
        pltpu.VMEM((steps, 7, rows, lanes), f32),
        pltpu.VMEM((4, rows, lanes), f32),
        pltpu.VMEM((2, 6, rows, lanes), f32),
        pltpu.SemaphoreType.DMA((2, steps)),
        pltpu.SemaphoreType.DMA((2, steps, len(CHUNKS))),
    ]


def split_step(nx, ny, fields, material, permittivity):
    _, cx, cy, cz = fields.shape
    f32 = jnp.float32
    x_lines = [pltpu.VMEM((cx, cy, cz), f32)] * 4
    y_lines = [pltpu.VMEM((cy, cx, cz), f32)] * 4
    result = pl.pallas_call(
        functools.partial(step_kernel, nx, ny, cx, cy, cz),
        out_shape=jax.ShapeDtypeStruct((6, cx * cy, cz), f32),
        in_specs=[
            pl.BlockSpec(memory_space=pl.ANY),
            pl.BlockSpec(memory_space=pltpu.VMEM),
            pl.BlockSpec(memory_space=pltpu.SMEM),
        ],
        out_specs=pl.BlockSpec(memory_space=pltpu.VMEM),
        scratch_shapes=[
            pltpu.VMEM((6, cx + 2, cy, cz), f32),
            pltpu.VMEM((6, (cy + 2) * cx, cz), f32),
            pltpu.VMEM((2, 4, cx, cz), f32),
            pltpu.VMEM((4, cx, cz), f32),
            pltpu.VMEM((4, cx, cz), f32),
            pltpu.VMEM((cx * cy, cz), f32),
            *x_lines,
            pltpu.VMEM((6, cx, cy, cz), f32),
            pltpu.VMEM((cy, cx, cz), f32),
            *y_lines,
            pltpu.VMEM((6, cy, cx, cz), f32),
            pltpu.SemaphoreType.DMA,
            pltpu.SemaphoreType.DMA((3, 4)),
            *line_scratch(nx, cy, cz),
            *line_scratch(ny, cx, cz),
        ],
        compiler_params=pltpu.CompilerParams(collective_id=0, has_side_effects=True),
        name="split_step",
    )(fields, material, permittivity)
    return result


def far_kernel(nx, ny, scale, cell_ref, new_ref, cell_col, owner_col, weight_ref, out_ref,
               rows_ref, parts, landed, send_sems, recv_sems):
    count = nx * ny
    me = lax.axis_index("gx") * ny + lax.axis_index("gy")
    barrier = pltpu.get_barrier_semaphore()

    def hello(k, carry):
        to = (me + k) % count
        pl.semaphore_signal(barrier, inc=1, device_id=(to // ny, to % ny), device_id_type=MESH)
        return carry

    lax.fori_loop(1, count, hello, 0)
    patches = cell_ref.shape[0]
    lanes = new_ref.shape[2]

    def fetch(q, carry):
        for u in range(8):
            p = q * 8 + u
            row = cell_ref[p] // lanes
            for m in range(6):
                rows_ref[m, pl.ds(p, 1), :] = new_ref[m, pl.ds(row, 1), :]
        return carry

    lax.fori_loop(0, patches // 8, fetch, 0)
    at = lax.broadcasted_iota(jnp.int32, (patches, lanes), 1)
    hit = at == (cell_col[...] & (lanes - 1))
    hot = (lax.broadcasted_iota(jnp.int32, (patches, count), 1) == owner_col[...]).astype(jnp.float32)
    angles = out_ref.shape[1]
    for m in range(6):
        value = jnp.sum(jnp.where(hit, rows_ref[m], 0.0), axis=1, keepdims=True)
        product = lax.dot_general(hot * value, weight_ref[...], (((0,), (0,)), ((), ())),
                                  precision=lax.Precision.HIGHEST,
                                  preferred_element_type=jnp.float32)
        for s in range(2):
            parts[pl.ds(s * 6 + m, count, stride=16), :] = product[:, s * angles:(s + 1) * angles]
    pl.semaphore_wait(barrier, count - 1)

    def piece(k):
        to = (me + k) % count
        return pltpu.make_async_remote_copy(
            parts.at[pl.ds(pl.multiple_of(to * 16, 16), 16)], landed.at[k],
            send_sems.at[k], recv_sems.at[k],
            device_id=(to // ny, to % ny), device_id_type=MESH)

    def send(k, carry):
        piece(k).start()
        return carry

    lax.fori_loop(1, count, send, 0)

    def add(k, total):
        piece(k).wait_recv()
        return total + landed[k]

    total = lax.fori_loop(1, count, add, parts[pl.ds(pl.multiple_of(me * 16, 16), 16), :])
    out_ref[...] = total[:12] * scale

    def done(k, carry):
        piece(k).wait_send()
        return carry

    lax.fori_loop(1, count, done, 0)


def far_sums(nx, ny, scale, new_flat, patch_cell, patch_owner, weights):
    count = nx * ny
    patches = patch_cell.shape[0]
    lanes = new_flat.shape[2]
    vmem = pl.BlockSpec(memory_space=pltpu.VMEM)
    return pl.pallas_call(
        functools.partial(far_kernel, nx, ny, scale),
        out_shape=jax.ShapeDtypeStruct((12, ANG_DEV), jnp.float32),
        in_specs=[pl.BlockSpec(memory_space=pltpu.SMEM), vmem, vmem, vmem, vmem],
        out_specs=vmem,
        scratch_shapes=[
            pltpu.VMEM((6, patches, lanes), jnp.float32),
            pltpu.VMEM((count * 16, ANG_DEV), jnp.float32),
            pltpu.VMEM((count, 16, ANG_DEV), jnp.float32),
            pltpu.SemaphoreType.DMA((count,)),
            pltpu.SemaphoreType.DMA((count,)),
        ],
        compiler_params=pltpu.CompilerParams(collective_id=1, has_side_effects=True),
        name="far_sums",
    )(patch_cell, new_flat, patch_cell[:, None], patch_owner, weights)


def far_phase(pos_x, pos_y, pos_z, owner_f, owners, angle_count):
    theta = math.pi * (jnp.arange(angle_count, dtype=jnp.float32) + 0.5) / angle_count
    azimuth = owner_f * (2.0 * math.pi / owners)
    sin_theta = jnp.sin(theta)[None, :]
    cos_theta = jnp.cos(theta)[None, :]
    cos_phi = jnp.cos(azimuth)[:, None]
    sin_phi = jnp.sin(azimuth)[:, None]
    return KAPPA * (
        pos_x[:, None] * sin_theta * cos_phi
        + pos_y[:, None] * sin_theta * sin_phi
        + pos_z[:, None] * cos_theta
    )


def local(nx, ny, fields, material, permittivity, patch_cell, patch_owner):
    _, cells_x, cells_y, cells_z = fields.shape
    grid_x = (lax.axis_index("gx") * cells_x + patch_cell // (cells_y * cells_z)).astype(jnp.float32)
    grid_y = (lax.axis_index("gy") * cells_y + patch_cell // cells_z % cells_y).astype(jnp.float32)
    grid_z = (patch_cell % cells_z).astype(jnp.float32)
    owner = patch_owner[:, 0].astype(jnp.float32)
    phases = far_phase(grid_x, grid_y, grid_z, owner, nx * ny, ANG_DEV)
    weights = jnp.concatenate([jnp.cos(phases), jnp.sin(phases)], axis=1)
    new_flat = split_step(nx, ny, fields, material, permittivity)
    scale = 1.0 / math.sqrt(patch_cell.shape[0])
    far_field = far_sums(nx, ny, scale, new_flat, patch_cell, patch_owner, weights)
    return new_flat.reshape(fields.shape), far_field


def solution(mesh):
    return jax.shard_map(
        functools.partial(local, mesh.shape["gx"], mesh.shape["gy"]),
        mesh=mesh,
        in_specs=(
            P(None, "gx", "gy", None),
            P("gx", "gy", None),
            P(),
            P(("gx", "gy")),
            P(("gx", "gy"), None),
        ),
        out_specs=(P(None, "gx", "gy", None), P(None, ("gx", "gy"))),
        check_vma=False,
    )
```

```python
import functools
import math

import jax
import jax.numpy as jnp
from jax import lax
from jax.experimental import pallas as pl
from jax.experimental.pallas import tpu as pltpu
from jax.sharding import PartitionSpec as P

ANG_DEV = 128
COURANT = 64
KAPPA = 0.5
MESH = pl.DeviceIdType.MESH
Y_MEMBERS = (0, 2, 3, 5)
CHUNKS = ((0, 2), (2, 2), (4, 2))


def slope_rows(value, low_row, high_row):
    rows = value.shape[0]
    at = lax.broadcasted_iota(jnp.int32, value.shape, 0)
    below = jnp.where(at == 0, low_row, pltpu.roll(value, 1, 0))
    above = jnp.where(at == rows - 1, high_row, pltpu.roll(value, rows - 1, 0))
    return 0.5 * (above - below)


def slope_lanes(value):
    lanes = value.shape[1]
    at = lax.broadcasted_iota(jnp.int32, value.shape, 1)
    below = jnp.where(at == 0, 0.0, pltpu.roll(value, 1, 1))
    above = jnp.where(at == lanes - 1, 0.0, pltpu.roll(value, lanes - 1, 1))
    return 0.5 * (above - below)


def updated(centre, slope_x, slope_y, curl_coef, half_step):
    slope_z = lambda member: slope_lanes(centre[member])
    curl_h = [slope_y(5) - slope_z(4), slope_z(3) - slope_x(5), slope_x(4) - slope_y(3)]
    curl_e = [slope_y(2) - slope_z(1), slope_z(0) - slope_x(2), slope_x(1) - slope_y(0)]
    return [centre[m] + curl_coef * curl_h[m] for m in range(3)] + [
        centre[3 + m] - half_step * curl_e[m] for m in range(3)
    ]


def factor(length, coef_at, gain_ref, pivot_ref, left_ref, right_ref):
    zero = jnp.zeros(gain_ref.shape[1:], jnp.float32)

    def forward(i, carry):
        gain_prev, left_prev = carry
        coef = coef_at(i)
        pivot = 1.0 / (1.0 + 2.0 * coef - coef * gain_prev)
        gain = coef * pivot
        left = gain * left_prev
        gain_ref[i] = gain
        pivot_ref[i] = pivot
        left_ref[i] = left
        return gain, left

    lax.fori_loop(0, length, forward, (zero, jnp.ones_like(zero)), unroll=2)

    def backward(k, carry):
        left_next, right_next = carry
        i = length - 1 - k
        gain = gain_ref[i]
        left = left_ref[i] + gain * left_next
        right = gain * right_next
        left_ref[i] = left
        right_ref[i] = right
        return left, right

    lax.fori_loop(0, length, backward, (zero, jnp.ones_like(zero)), unroll=4)


def sweep_back(length, gain_ref, solved_ref):
    def backward(k, carry):
        i = length - 1 - k
        gain = gain_ref[i]
        now = [solved_ref[m, i] + gain * carry[m] for m in range(6)]
        for m in range(6):
            solved_ref[m, i] = now[m]
        return tuple(now)

    zero = jnp.zeros(gain_ref.shape[1:], jnp.float32)
    lax.fori_loop(0, length, backward, (zero,) * 6, unroll=4)


class Line:
    def __init__(self, axis, count, refs):
        (self.mat_out, self.mat_in, self.rhs_out, self.rhs_in, self.plan, self.gains, self.ends,
         self.mat_sems, self.rhs_sems) = refs
        self.axis = axis
        self.count = count
        self.steps = count.bit_length() - 1
        self.me = lax.axis_index(axis)

    def near(self, k):
        return 1 - (self.me // 2**k) % 2

    def partner(self, k):
        return {self.axis: self.me + (2 * self.near(k) - 1) * 2**k}

    def mat_copy(self, k):
        return pltpu.make_async_remote_copy(
            self.mat_out.at[k], self.mat_in.at[k], self.mat_sems.at[0, k], self.mat_sems.at[1, k],
            device_id=self.partner(k), device_id_type=MESH)

    def rhs_copy(self, k, j):
        first, size = CHUNKS[j]
        if k == self.steps - 1:
            source = self.rhs_out.at[k, self.near(k), pl.ds(first, size)]
            target = self.rhs_in.at[k, 0, pl.ds(first, size)]
        else:
            source = self.rhs_out.at[k, :, pl.ds(first, size)]
            target = self.rhs_in.at[k, :, pl.ds(first, size)]
        return pltpu.make_async_remote_copy(
            source, target, self.rhs_sems.at[0, k, j], self.rhs_sems.at[1, k, j],
            device_id=self.partner(k), device_id_type=MESH)

    def mat_start(self, left_ref, right_ref):
        last = left_ref.shape[0] - 1
        for end, at in ((0, 0), (1, last)):
            self.mat_out[0, 2 * end] = left_ref[at]
            self.mat_out[0, 2 * end + 1] = right_ref[at]
        one, zero = jnp.ones(left_ref.shape[1:], jnp.float32), jnp.zeros(left_ref.shape[1:], jnp.float32)
        self.gains[0] = one
        self.gains[1] = zero
        self.gains[2] = zero
        self.gains[3] = one
        self.mat_copy(0).start()

    def mat_merge(self, k):
        self.mat_copy(k).wait_recv()
        n = self.near(k)
        f = 1 - n
        mine = lambda end, side: self.mat_out[k, 2 * end + side]
        other = lambda end, side: self.mat_in[k, 2 * end + side]
        m_nn, m_fn, m_nf, m_ff = mine(n, n), mine(f, n), mine(n, f), mine(f, f)
        o_nn, o_fn, o_nf, o_ff = other(f, f), other(n, f), other(f, n), other(n, n)
        inv = 1.0 / (1.0 - m_nn * o_nn)
        o_by_m = o_nn * m_nf * inv
        o_by_o = o_nf * inv
        m_by_m = m_nf * inv
        m_by_o = m_nn * o_nf * inv
        gain_in, gain_out = self.gains[n], self.gains[2 + n]
        for slot, value in enumerate((inv, o_nn * inv, m_nn * inv, m_fn, o_fn, gain_in, gain_out)):
            self.plan[k, slot] = value
        if k < self.steps - 1:
            self.mat_out[k + 1, 2 * f + f] = m_ff + m_fn * o_by_m
            self.mat_out[k + 1, 2 * f + n] = m_fn * o_by_o
            self.mat_out[k + 1, 2 * n + n] = o_ff + o_fn * m_by_o
            self.mat_out[k + 1, 2 * n + f] = o_fn * m_by_m
            self.mat_copy(k + 1).start()
            self.gains[f] = self.gains[f] + gain_in * o_by_m
            self.gains[2 + f] = self.gains[2 + f] + gain_out * o_by_m
            self.gains[n] = gain_in * o_by_o
            self.gains[2 + n] = gain_out * o_by_o

    def rhs_start(self, solved_ref):
        last = solved_ref.shape[1] - 1
        for j, (first, size) in enumerate(CHUNKS):
            for m in range(first, first + size):
                self.rhs_out[0, 0, m] = solved_ref[m, 0]
                self.rhs_out[0, 1, m] = solved_ref[m, last]
            self.rhs_copy(0, j).start()

    def rhs_merge(self, k, j):
        first, size = CHUNKS[j]
        self.rhs_copy(k, j).wait_recv()
        n = self.near(k)
        f = 1 - n
        ending = k == self.steps - 1
        inv, o_nn, m_nn, m_fn, o_fn, gain_in, gain_out = [self.plan[k, slot] for slot in range(7)]
        for m in range(first, first + size):
            mine = self.rhs_out[k, n, m]
            other = self.rhs_in[k, 0, m] if ending else self.rhs_in[k, f, m]
            o_value = other * inv + o_nn * mine
            if not ending:
                m_value = mine * inv + m_nn * other
                self.rhs_out[k + 1, f, m] = self.rhs_out[k, f, m] + m_fn * o_value
                self.rhs_out[k + 1, n, m] = self.rhs_in[k, n, m] + o_fn * m_value
            into, out_of = gain_in * o_value, gain_out * o_value
            if k > 0:
                into, out_of = self.ends[0, m] + into, self.ends[1, m] + out_of
            self.ends[0, m] = into
            self.ends[1, m] = out_of
        if not ending:
            self.rhs_copy(k + 1, j).start()

    def drain(self):
        for k in range(self.steps):
            self.mat_copy(k).wait_send()
            for j in range(len(CHUNKS)):
                self.rhs_copy(k, j).wait_send()


def both_ways(axis, count, out_low, out_high, in_low, in_high, sems):
    me = lax.axis_index(axis)
    up = lambda: pltpu.make_async_remote_copy(
        out_high, in_low, sems.at[0], sems.at[1], device_id={axis: me + 1}, device_id_type=MESH)
    down = lambda: pltpu.make_async_remote_copy(
        out_low, in_high, sems.at[2], sems.at[3], device_id={axis: me - 1}, device_id_type=MESH)

    def start():
        @pl.when(me < count - 1)
        def _():
            up().start()

        @pl.when(me > 0)
        def _():
            down().start()

        @pl.when(me == 0)
        def _():
            in_low[...] = jnp.zeros(in_low.shape, jnp.float32)

        @pl.when(me == count - 1)
        def _():
            in_high[...] = jnp.zeros(in_high.shape, jnp.float32)

    def wait():
        @pl.when(me > 0)
        def _():
            up().wait_recv()

        @pl.when(me < count - 1)
        def _():
            down().wait_recv()

    def drain():
        @pl.when(me < count - 1)
        def _():
            up().wait_send()

        @pl.when(me > 0)
        def _():
            down().wait_send()

    return start, wait, drain


def greet_all(count, ny, me, barrier):
    def hello(k, carry):
        to = (me + k) % count
        pl.semaphore_signal(barrier, inc=1, device_id=(to // ny, to % ny), device_id_type=MESH)
        return carry

    lax.fori_loop(1, count, hello, 0)


def cos_sin(angle):
    turns = jnp.floor(angle * (2.0 / math.pi) + 0.5)
    rest = ((angle - turns * 1.5703125) - turns * 4.837512969970703125e-4) - turns * 7.54978995489188216e-8
    square = rest * rest
    sine = ((-1.9515295891e-4 * square + 8.3321608736e-3) * square - 1.6666654611e-1) * square * rest + rest
    cosine = (
        (2.443315711809948e-5 * square - 1.388731625493765e-3) * square + 4.166664568298827e-2
    ) * square * square - 0.5 * square + 1.0
    quarter = turns.astype(jnp.int32) & 3
    swap = (quarter & 1) == 1
    plain_cos = jnp.where(swap, sine, cosine)
    plain_sin = jnp.where(swap, cosine, sine)
    minus_cos = (quarter == 1) | (quarter == 2)
    return jnp.where(minus_cos, -plain_cos, plain_cos), jnp.where(quarter >= 2, -plain_sin, plain_sin)


def fill_weights(count, cx, cy, cz, cell_row, owner_row, weight_ref):
    angles = weight_ref.shape[0] // 2
    cell = cell_row[...]
    bits = cz.bit_length() - 1
    line = lax.shift_right_logical(cell, jnp.full_like(cell, bits))
    at_x = jnp.zeros_like(cell)
    for i in range(1, cx):
        at_x = at_x + jnp.where(line >= i * cy, 1, 0)
    at_y = line - at_x * cy
    pos_x = (at_x + lax.axis_index("gx") * cx).astype(jnp.float32)
    pos_y = (at_y + lax.axis_index("gy") * cy).astype(jnp.float32)
    pos_z = (cell - line * cz).astype(jnp.float32)
    cos_phi, sin_phi = cos_sin(owner_row[...].astype(jnp.float32) * (2.0 * math.pi / count))
    shape = (8, cell.shape[1])
    wide = [jnp.broadcast_to(v, shape) for v in (pos_x, pos_y, pos_z, cos_phi, sin_phi)]

    def group(g, carry):
        pos_x, pos_y, pos_z, cos_phi, sin_phi = carry
        start = pl.multiple_of(g * 8, 8)
        index = (lax.broadcasted_iota(jnp.int32, shape, 0) + start).astype(jnp.float32)
        cos_theta, sin_theta = cos_sin(math.pi * (index + 0.5) / angles)
        phase = KAPPA * (pos_x * sin_theta * cos_phi + pos_y * sin_theta * sin_phi + pos_z * cos_theta)
        cosine, sine = cos_sin(phase)
        weight_ref[pl.ds(start, 8), :] = cosine
        weight_ref[pl.ds(start + angles, 8), :] = sine
        return carry

    lax.fori_loop(0, angles // 8, group, tuple(wide))


def step_kernel(nx, ny, cx, cy, cz, scale, fields_hbm, material_ref, permit_ref, cell_smem,
                cell_row, owner_row, out_ref, far_ref,
                grid_x, grid_y, y_out, y_low, y_high, coef_x,
                gain_x, pivot_x, left_x, right_x, solved_x,
                coef_y, gain_y, pivot_y, left_y, right_y, solved_y,
                weight_ref, packed, samples, spread, parts, landed,
                load_sem, halo_sems, part_sems, *line_refs):
    half_step = COURANT / 2.0
    count = nx * ny
    me = lax.axis_index("gx") * ny + lax.axis_index("gy")
    barrier = pltpu.get_barrier_semaphore()
    load = pltpu.make_async_copy(fields_hbm, grid_x.at[:, pl.ds(1, cx)], load_sem)
    load.start()
    greet_all(count, ny, me, barrier)
    line_x = Line("gx", nx, line_refs[:9])
    line_y = Line("gy", ny, line_refs[9:])

    x_halo = both_ways("gx", nx, grid_x.at[pl.ds(1, 5), 1], grid_x.at[pl.ds(1, 5), cx],
                       grid_x.at[pl.ds(1, 5), 0], grid_x.at[pl.ds(1, 5), cx + 1], halo_sems.at[0])
    y_halo = both_ways("gy", ny, y_out.at[0], y_out.at[1], y_low, y_high, halo_sems.at[1])
    mid_halo = both_ways("gy", ny, grid_y.at[:, pl.ds(cx, cx)], grid_y.at[:, pl.ds(cx * cy, cx)],
                         grid_y.at[:, pl.ds(0, cx)], grid_y.at[:, pl.ds(cx * (cy + 1), cx)],
                         halo_sems.at[2])

    def coefs(i, carry):
        which = material_ref[i]
        permit = jnp.zeros(which.shape, jnp.float32)
        for entry in range(permit_ref.shape[0]):
            permit = jnp.where(which == entry, permit_ref[entry], permit)
        coef_x[pl.ds(pl.multiple_of(i * cy, 8), cy), :] = (half_step * half_step) / permit
        return carry

    lax.fori_loop(0, cx, coefs, 0, unroll=2)
    load.wait()
    for slot, member in enumerate(Y_MEMBERS):
        y_out[0, slot] = jnp.concatenate([grid_x[member, 1 + i, 0:1] for i in range(cx)], axis=0)
        y_out[1, slot] = jnp.concatenate([grid_x[member, 1 + i, cy - 1:cy] for i in range(cx)], axis=0)
    pl.semaphore_wait(barrier, count - 1)
    x_halo[0]()
    y_halo[0]()
    coef_plane = lambda i: coef_x[pl.ds(pl.multiple_of(i * cy, 8), cy), :]
    factor(cx, coef_plane, gain_x, pivot_x, left_x, right_x)
    line_x.mat_start(left_x, right_x)
    for j in range(cy):
        coef_y[j] = coef_x[pl.ds(j, cx, stride=cy), :]
    x_halo[1]()
    y_halo[1]()
    y_slot = {member: slot for slot, member in enumerate(Y_MEMBERS)}

    def forward_x(i, carry):
        centre = [grid_x[m, i + 1] for m in range(6)]
        slope_x = lambda m: 0.5 * (grid_x[m, i + 2] - grid_x[m, i])
        slope_y = lambda m: slope_rows(
            centre[m], y_low[y_slot[m], pl.ds(i, 1), :], y_high[y_slot[m], pl.ds(i, 1), :])
        right = updated(centre, slope_x, slope_y, coef_plane(i) * (1.0 / half_step), half_step)
        gain, pivot = gain_x[i], pivot_x[i]
        now = [right[m] * pivot + gain * carry[m] for m in range(6)]
        for m in range(6):
            solved_x[m, i] = now[m]
        return tuple(now)

    lax.fori_loop(0, cx, forward_x, (jnp.zeros((cy, cz), jnp.float32),) * 6)
    early = min(2, line_x.steps)
    line_x.mat_merge(0)
    sweep_back(cx, gain_x, solved_x)
    line_x.rhs_start(solved_x)
    if early > 1:
        line_x.mat_merge(1)
    factor(cy, lambda j: coef_y[j], gain_y, pivot_y, left_y, right_y)
    line_y.mat_start(left_y, right_y)
    for k in range(line_x.steps):
        if k >= early:
            line_x.mat_merge(k)
        for j in range(len(CHUNKS)):
            line_x.rhs_merge(k, j)
        if k < line_y.steps:
            line_y.mat_merge(k)
    for k in range(line_x.steps, line_y.steps):
        line_y.mat_merge(k)

    for i in range(cx):
        left, right = left_x[i], right_x[i]
        for m in range(6):
            grid_y[m, pl.ds(cx + i, cy, stride=cx), :] = (
                solved_x[m, i] + left * line_x.ends[0, m] + right * line_x.ends[1, m])
    mid_halo[0]()
    fill_weights(count, cx, cy, cz, cell_row, owner_row, weight_ref)
    mid_halo[1]()

    y_plane = lambda m, j: grid_y[m, pl.ds(pl.multiple_of(j * cx, 8), cx), :]

    def forward_y(j, carry):
        centre = [y_plane(m, j + 1) for m in range(6)]
        slope_y = lambda m: 0.5 * (y_plane(m, j + 2) - y_plane(m, j))
        slope_x = lambda m: slope_rows(
            centre[m], line_x.ends[0, m, pl.ds(j, 1), :], line_x.ends[1, m, pl.ds(j, 1), :])
        right = updated(centre, slope_x, slope_y, coef_y[j] * (1.0 / half_step), half_step)
        gain, pivot = gain_y[j], pivot_y[j]
        now = [right[m] * pivot + gain * carry[m] for m in range(6)]
        for m in range(6):
            solved_y[m, j] = now[m]
        return tuple(now)

    lax.fori_loop(0, cy, forward_y, (jnp.zeros((cx, cz), jnp.float32),) * 6, unroll=2)
    sweep_back(cy, gain_y, solved_y)
    line_y.rhs_start(solved_y)
    for k in range(line_y.steps):
        for j in range(len(CHUNKS)):
            line_y.rhs_merge(k, j)
    for j in range(cy):
        left, right = left_y[j], right_y[j]
        for m in range(6):
            value = solved_y[m, j] + left * line_y.ends[0, m] + right * line_y.ends[1, m]
            out_ref[m, pl.ds(j, cx, stride=cy), :] = value
            packed[pl.ds(j * 8 + m, cx, stride=cy * 8), :] = value

    patches = cell_smem.shape[0]

    def fetch(q, carry):
        for u in range(8):
            p = q * 8 + u
            line = cell_smem[p] // cz
            samples[pl.ds(p, 8, stride=patches), :] = packed[pl.ds(line * 8, 8), :]
        return carry

    lax.fori_loop(0, patches // 8, fetch, 0)
    spot = jnp.transpose(jnp.broadcast_to(cell_row[...] & (cz - 1), (cz, patches)))
    hit = lax.broadcasted_iota(jnp.int32, (patches, cz), 1) == spot
    column = lax.broadcasted_iota(jnp.int32, (patches, 128), 1)
    table = jnp.zeros((patches, 128), jnp.float32)
    for m in range(6):
        value = jnp.sum(jnp.where(hit, samples[pl.ds(m * patches, patches), :], 0.0), axis=1, keepdims=True)
        table = jnp.where(column == m, value, table)
    values = jnp.transpose(table)
    owner = owner_row[...]
    hot = (lax.broadcasted_iota(jnp.int32, (count, patches), 0) == owner).astype(jnp.float32)
    for m in range(6):
        spread[pl.ds(m * count, count), :] = hot * values[m:m + 1]
    product = lax.dot_general(spread[...], weight_ref[...], (((1,), (1,)), ((), ())),
                              precision=lax.Precision.HIGHEST, preferred_element_type=jnp.float32)
    angles = far_ref.shape[1]
    for m in range(6):
        for s in range(2):
            parts[pl.ds(s * 6 + m, count, stride=16), :] = (
                product[m * count:(m + 1) * count, s * angles:(s + 1) * angles])

    def piece(k):
        to = (me + k) % count
        return pltpu.make_async_remote_copy(
            parts.at[pl.ds(pl.multiple_of(to * 16, 16), 16)], landed.at[k],
            part_sems.at[0, k], part_sems.at[1, k],
            device_id=(to // ny, to % ny), device_id_type=MESH)

    def send(k, carry):
        piece(k).start()
        return carry

    lax.fori_loop(1, count, send, 0)
    for halo in (x_halo, y_halo, mid_halo):
        halo[2]()
    line_x.drain()
    line_y.drain()

    def add(k, total):
        piece(k).wait_recv()
        return total + landed[k]

    total = lax.fori_loop(1, count, add, parts[pl.ds(pl.multiple_of(me * 16, 16), 16), :])
    far_ref[...] = total[:12] * scale

    def done(k, carry):
        piece(k).wait_send()
        return carry

    lax.fori_loop(1, count, done, 0)


def line_scratch(count, rows, lanes):
    steps = count.bit_length() - 1
    f32 = jnp.float32
    return [
        pltpu.VMEM((steps, 4, rows, lanes), f32),
        pltpu.VMEM((steps, 4, rows, lanes), f32),
        pltpu.VMEM((steps, 2, 6, rows, lanes), f32),
        pltpu.VMEM((steps, 2, 6, rows, lanes), f32),
        pltpu.VMEM((steps, 7, rows, lanes), f32),
        pltpu.VMEM((4, rows, lanes), f32),
        pltpu.VMEM((2, 6, rows, lanes), f32),
        pltpu.SemaphoreType.DMA((2, steps)),
        pltpu.SemaphoreType.DMA((2, steps, len(CHUNKS))),
    ]


def local(nx, ny, fields, material, permittivity, patch_cell, patch_owner):
    _, cx, cy, cz = fields.shape
    f32 = jnp.float32
    count = nx * ny
    patches = patch_cell.shape[0]
    vmem = pl.BlockSpec(memory_space=pltpu.VMEM)
    smem = pl.BlockSpec(memory_space=pltpu.SMEM)
    x_lines = [pltpu.VMEM((cx, cy, cz), f32)] * 4
    y_lines = [pltpu.VMEM((cy, cx, cz), f32)] * 4
    new_flat, far_field = pl.pallas_call(
        functools.partial(step_kernel, nx, ny, cx, cy, cz, 1.0 / math.sqrt(patches)),
        out_shape=(
            jax.ShapeDtypeStruct((6, cx * cy, cz), f32),
            jax.ShapeDtypeStruct((12, ANG_DEV), f32),
        ),
        in_specs=[pl.BlockSpec(memory_space=pltpu.HBM), vmem, smem, smem, vmem, vmem],
        out_specs=(vmem, vmem),
        scratch_shapes=[
            pltpu.VMEM((6, cx + 2, cy, cz), f32),
            pltpu.VMEM((6, (cy + 2) * cx, cz), f32),
            pltpu.VMEM((2, 4, cx, cz), f32),
            pltpu.VMEM((4, cx, cz), f32),
            pltpu.VMEM((4, cx, cz), f32),
            pltpu.VMEM((cx * cy, cz), f32),
            *x_lines,
            pltpu.VMEM((6, cx, cy, cz), f32),
            pltpu.VMEM((cy, cx, cz), f32),
            *y_lines,
            pltpu.VMEM((6, cy, cx, cz), f32),
            pltpu.VMEM((2 * ANG_DEV, patches), f32),
            pltpu.VMEM((cx * cy * 8, cz), f32),
            pltpu.VMEM((8 * patches, cz), f32),
            pltpu.VMEM((6 * count, patches), f32),
            pltpu.VMEM((count * 16, ANG_DEV), f32),
            pltpu.VMEM((count, 16, ANG_DEV), f32),
            pltpu.SemaphoreType.DMA,
            pltpu.SemaphoreType.DMA((3, 4)),
            pltpu.SemaphoreType.DMA((2, count)),
            *line_scratch(nx, cy, cz),
            *line_scratch(ny, cx, cz),
        ],
        compiler_params=pltpu.CompilerParams(
            collective_id=0, has_side_effects=True, vmem_limit_bytes=40 * 2**20),
        name="split_step",
    )(fields, material, permittivity, patch_cell, patch_cell[None, :], patch_owner.reshape(1, patches))
    return new_flat.reshape(fields.shape), far_field


def solution(mesh):
    return jax.shard_map(
        functools.partial(local, mesh.shape["gx"], mesh.shape["gy"]),
        mesh=mesh,
        in_specs=(
            P(None, "gx", "gy", None),
            P("gx", "gy", None),
            P(),
            P(("gx", "gy")),
            P(("gx", "gy"), None),
        ),
        out_specs=(P(None, "gx", "gy", None), P(None, ("gx", "gy"))),
        check_vma=False,
    )
```

```python
import functools
import math

import jax
import jax.numpy as jnp
from jax import lax
from jax.experimental import pallas as pl
from jax.experimental.pallas import tpu as pltpu
from jax.sharding import PartitionSpec as P

ANG_DEV = 128
COURANT = 64
KAPPA = 0.5
MESH = pl.DeviceIdType.MESH
Y_MEMBERS = (0, 2, 3, 5)
CHUNKS = ((0, 2), (2, 2), (4, 2))


def slope_rows(value, low_row, high_row):
    rows = value.shape[0]
    at = lax.broadcasted_iota(jnp.int32, value.shape, 0)
    below = jnp.where(at == 0, low_row, pltpu.roll(value, 1, 0))
    above = jnp.where(at == rows - 1, high_row, pltpu.roll(value, rows - 1, 0))
    return 0.5 * (above - below)


def slope_lanes(value):
    lanes = value.shape[1]
    at = lax.broadcasted_iota(jnp.int32, value.shape, 1)
    below = jnp.where(at == 0, 0.0, pltpu.roll(value, 1, 1))
    above = jnp.where(at == lanes - 1, 0.0, pltpu.roll(value, lanes - 1, 1))
    return 0.5 * (above - below)


def updated(centre, slope_x, slope_y, curl_coef, half_step):
    slope_z = lambda member: slope_lanes(centre[member])
    curl_h = [slope_y(5) - slope_z(4), slope_z(3) - slope_x(5), slope_x(4) - slope_y(3)]
    curl_e = [slope_y(2) - slope_z(1), slope_z(0) - slope_x(2), slope_x(1) - slope_y(0)]
    return [centre[m] + curl_coef * curl_h[m] for m in range(3)] + [
        centre[3 + m] - half_step * curl_e[m] for m in range(3)
    ]


def factor(length, coef_at, gain_ref, pivot_ref, left_ref, right_ref):
    zero = jnp.zeros(gain_ref.shape[1:], jnp.float32)

    def forward(i, carry):
        gain_prev, left_prev = carry
        coef = coef_at(i)
        pivot = 1.0 / (1.0 + 2.0 * coef - coef * gain_prev)
        gain = coef * pivot
        left = gain * left_prev
        gain_ref[i] = gain
        pivot_ref[i] = pivot
        left_ref[i] = left
        return gain, left

    lax.fori_loop(0, length, forward, (zero, jnp.ones_like(zero)), unroll=2)

    def backward(k, carry):
        left_next, right_next = carry
        i = length - 1 - k
        gain = gain_ref[i]
        left = left_ref[i] + gain * left_next
        right = gain * right_next
        left_ref[i] = left
        right_ref[i] = right
        return left, right

    lax.fori_loop(0, length, backward, (zero, jnp.ones_like(zero)), unroll=4)


def sweep_back(length, gain_ref, solved_ref):
    def backward(k, carry):
        i = length - 1 - k
        gain = gain_ref[i]
        now = [solved_ref[m, i] + gain * carry[m] for m in range(6)]
        for m in range(6):
            solved_ref[m, i] = now[m]
        return tuple(now)

    zero = jnp.zeros(gain_ref.shape[1:], jnp.float32)
    lax.fori_loop(0, length, backward, (zero,) * 6, unroll=4)


class Line:
    def __init__(self, axis, count, refs):
        (self.mat_out, self.mat_in, self.rhs_out, self.rhs_in, self.plan, self.gains, self.ends,
         self.mat_sems, self.rhs_sems) = refs
        self.axis = axis
        self.count = count
        self.steps = count.bit_length() - 1
        self.me = lax.axis_index(axis)

    def near(self, k):
        return 1 - (self.me // 2**k) % 2

    def partner(self, k):
        return {self.axis: self.me + (2 * self.near(k) - 1) * 2**k}

    def mat_copy(self, k):
        return pltpu.make_async_remote_copy(
            self.mat_out.at[k], self.mat_in.at[k], self.mat_sems.at[0, k], self.mat_sems.at[1, k],
            device_id=self.partner(k), device_id_type=MESH)

    def rhs_copy(self, k, j):
        first, size = CHUNKS[j]
        if k == self.steps - 1:
            source = self.rhs_out.at[k, self.near(k), pl.ds(first, size)]
            target = self.rhs_in.at[k, 0, pl.ds(first, size)]
        else:
            source = self.rhs_out.at[k, :, pl.ds(first, size)]
            target = self.rhs_in.at[k, :, pl.ds(first, size)]
        return pltpu.make_async_remote_copy(
            source, target, self.rhs_sems.at[0, k, j], self.rhs_sems.at[1, k, j],
            device_id=self.partner(k), device_id_type=MESH)

    def mat_start(self, left_ref, right_ref):
        last = left_ref.shape[0] - 1
        for end, at in ((0, 0), (1, last)):
            self.mat_out[0, 2 * end] = left_ref[at]
            self.mat_out[0, 2 * end + 1] = right_ref[at]
        one, zero = jnp.ones(left_ref.shape[1:], jnp.float32), jnp.zeros(left_ref.shape[1:], jnp.float32)
        self.gains[0] = one
        self.gains[1] = zero
        self.gains[2] = zero
        self.gains[3] = one
        self.mat_copy(0).start()

    def mat_merge(self, k):
        self.mat_copy(k).wait_recv()
        n = self.near(k)
        f = 1 - n
        mine = lambda end, side: self.mat_out[k, 2 * end + side]
        other = lambda end, side: self.mat_in[k, 2 * end + side]
        m_nn, m_fn, m_nf, m_ff = mine(n, n), mine(f, n), mine(n, f), mine(f, f)
        o_nn, o_fn, o_nf, o_ff = other(f, f), other(n, f), other(f, n), other(n, n)
        inv = 1.0 / (1.0 - m_nn * o_nn)
        o_by_m = o_nn * m_nf * inv
        o_by_o = o_nf * inv
        m_by_m = m_nf * inv
        m_by_o = m_nn * o_nf * inv
        gain_in, gain_out = self.gains[n], self.gains[2 + n]
        for slot, value in enumerate((inv, o_nn * inv, m_nn * inv, m_fn, o_fn, gain_in, gain_out)):
            self.plan[k, slot] = value
        if k < self.steps - 1:
            self.mat_out[k + 1, 2 * f + f] = m_ff + m_fn * o_by_m
            self.mat_out[k + 1, 2 * f + n] = m_fn * o_by_o
            self.mat_out[k + 1, 2 * n + n] = o_ff + o_fn * m_by_o
            self.mat_out[k + 1, 2 * n + f] = o_fn * m_by_m
            self.mat_copy(k + 1).start()
            self.gains[f] = self.gains[f] + gain_in * o_by_m
            self.gains[2 + f] = self.gains[2 + f] + gain_out * o_by_m
            self.gains[n] = gain_in * o_by_o
            self.gains[2 + n] = gain_out * o_by_o

    def rhs_start(self, solved_ref):
        last = solved_ref.shape[1] - 1
        for j, (first, size) in enumerate(CHUNKS):
            for m in range(first, first + size):
                self.rhs_out[0, 0, m] = solved_ref[m, 0]
                self.rhs_out[0, 1, m] = solved_ref[m, last]
            self.rhs_copy(0, j).start()

    def rhs_merge(self, k, j):
        first, size = CHUNKS[j]
        self.rhs_copy(k, j).wait_recv()
        n = self.near(k)
        f = 1 - n
        ending = k == self.steps - 1
        inv, o_nn, m_nn, m_fn, o_fn, gain_in, gain_out = [self.plan[k, slot] for slot in range(7)]
        for m in range(first, first + size):
            mine = self.rhs_out[k, n, m]
            other = self.rhs_in[k, 0, m] if ending else self.rhs_in[k, f, m]
            o_value = other * inv + o_nn * mine
            if not ending:
                m_value = mine * inv + m_nn * other
                self.rhs_out[k + 1, f, m] = self.rhs_out[k, f, m] + m_fn * o_value
                self.rhs_out[k + 1, n, m] = self.rhs_in[k, n, m] + o_fn * m_value
            into, out_of = gain_in * o_value, gain_out * o_value
            if k > 0:
                into, out_of = self.ends[0, m] + into, self.ends[1, m] + out_of
            self.ends[0, m] = into
            self.ends[1, m] = out_of
        if not ending:
            self.rhs_copy(k + 1, j).start()

    def drain(self):
        for k in range(self.steps):
            self.mat_copy(k).wait_send()
            for j in range(len(CHUNKS)):
                self.rhs_copy(k, j).wait_send()


def both_ways(axis, count, out_low, out_high, in_low, in_high, sems):
    me = lax.axis_index(axis)
    up = lambda: pltpu.make_async_remote_copy(
        out_high, in_low, sems.at[0], sems.at[1], device_id={axis: me + 1}, device_id_type=MESH)
    down = lambda: pltpu.make_async_remote_copy(
        out_low, in_high, sems.at[2], sems.at[3], device_id={axis: me - 1}, device_id_type=MESH)

    def start():
        @pl.when(me < count - 1)
        def _():
            up().start()

        @pl.when(me > 0)
        def _():
            down().start()

        @pl.when(me == 0)
        def _():
            in_low[...] = jnp.zeros(in_low.shape, jnp.float32)

        @pl.when(me == count - 1)
        def _():
            in_high[...] = jnp.zeros(in_high.shape, jnp.float32)

    def wait():
        @pl.when(me > 0)
        def _():
            up().wait_recv()

        @pl.when(me < count - 1)
        def _():
            down().wait_recv()

    def drain():
        @pl.when(me < count - 1)
        def _():
            up().wait_send()

        @pl.when(me > 0)
        def _():
            down().wait_send()

    return start, wait, drain


def greet_all(count, ny, me, barrier):
    def hello(k, carry):
        to = (me + k) % count
        pl.semaphore_signal(barrier, inc=1, device_id=(to // ny, to % ny), device_id_type=MESH)
        return carry

    lax.fori_loop(1, count, hello, 0)


def cos_sin(angle):
    turns = jnp.floor(angle * (2.0 / math.pi) + 0.5)
    rest = ((angle - turns * 1.5703125) - turns * 4.837512969970703125e-4) - turns * 7.54978995489188216e-8
    square = rest * rest
    sine = ((-1.9515295891e-4 * square + 8.3321608736e-3) * square - 1.6666654611e-1) * square * rest + rest
    cosine = (
        (2.443315711809948e-5 * square - 1.388731625493765e-3) * square + 4.166664568298827e-2
    ) * square * square - 0.5 * square + 1.0
    quarter = turns.astype(jnp.int32) & 3
    swap = (quarter & 1) == 1
    plain_cos = jnp.where(swap, sine, cosine)
    plain_sin = jnp.where(swap, cosine, sine)
    minus_cos = (quarter == 1) | (quarter == 2)
    return jnp.where(minus_cos, -plain_cos, plain_cos), jnp.where(quarter >= 2, -plain_sin, plain_sin)


def fill_weights(count, cx, cy, cz, cell_row, owner_row, weight_ref):
    angles = weight_ref.shape[0] // 2
    cell = cell_row[...]
    bits = cz.bit_length() - 1
    line = lax.shift_right_logical(cell, jnp.full_like(cell, bits))
    at_x = jnp.zeros_like(cell)
    for i in range(1, cx):
        at_x = at_x + jnp.where(line >= i * cy, 1, 0)
    at_y = line - at_x * cy
    pos_x = (at_x + lax.axis_index("gx") * cx).astype(jnp.float32)
    pos_y = (at_y + lax.axis_index("gy") * cy).astype(jnp.float32)
    pos_z = (cell - line * cz).astype(jnp.float32)
    cos_phi, sin_phi = cos_sin(owner_row[...].astype(jnp.float32) * (2.0 * math.pi / count))
    shape = (8, cell.shape[1])
    wide = [jnp.broadcast_to(v, shape) for v in (pos_x, pos_y, pos_z, cos_phi, sin_phi)]

    def group(g, carry):
        pos_x, pos_y, pos_z, cos_phi, sin_phi = carry
        start = pl.multiple_of(g * 8, 8)
        index = (lax.broadcasted_iota(jnp.int32, shape, 0) + start).astype(jnp.float32)
        cos_theta, sin_theta = cos_sin(math.pi * (index + 0.5) / angles)
        phase = KAPPA * (pos_x * sin_theta * cos_phi + pos_y * sin_theta * sin_phi + pos_z * cos_theta)
        cosine, sine = cos_sin(phase)
        weight_ref[pl.ds(start, 8), :] = cosine
        weight_ref[pl.ds(start + angles, 8), :] = sine
        return carry

    lax.fori_loop(0, angles // 8, group, tuple(wide))


def step_kernel(nx, ny, cx, cy, cz, scale, fields_hbm, material_hbm, permit_ref, cell_smem,
                cell_row, owner_row, new_hbm, far_ref, material_ref, out_ref,
                grid_x, grid_y, y_out, y_low, y_high, coef_x,
                gain_x, pivot_x, left_x, right_x, solved_x,
                coef_y, gain_y, pivot_y, left_y, right_y, solved_y,
                weight_ref, packed, samples, spread, parts, landed,
                load_sem, move_sems, halo_sems, part_sems, *line_refs):
    half_step = COURANT / 2.0
    count = nx * ny
    me = lax.axis_index("gx") * ny + lax.axis_index("gy")
    barrier = pltpu.get_barrier_semaphore()
    load = pltpu.make_async_copy(fields_hbm, grid_x.at[:, pl.ds(1, cx)], load_sem)
    load.start()
    load_material = pltpu.make_async_copy(material_hbm, material_ref, move_sems.at[0])
    load_material.start()
    greet_all(count, ny, me, barrier)
    line_x = Line("gx", nx, line_refs[:9])
    line_y = Line("gy", ny, line_refs[9:])

    x_halo = both_ways("gx", nx, grid_x.at[pl.ds(1, 5), 1], grid_x.at[pl.ds(1, 5), cx],
                       grid_x.at[pl.ds(1, 5), 0], grid_x.at[pl.ds(1, 5), cx + 1], halo_sems.at[0])
    y_halo = both_ways("gy", ny, y_out.at[0], y_out.at[1], y_low, y_high, halo_sems.at[1])
    mid_halo = both_ways("gy", ny, grid_y.at[:, pl.ds(cx, cx)], grid_y.at[:, pl.ds(cx * cy, cx)],
                         grid_y.at[:, pl.ds(0, cx)], grid_y.at[:, pl.ds(cx * (cy + 1), cx)],
                         halo_sems.at[2])

    def coefs(i, carry):
        which = material_ref[i]
        permit = jnp.zeros(which.shape, jnp.float32)
        for entry in range(permit_ref.shape[0]):
            permit = jnp.where(which == entry, permit_ref[entry], permit)
        coef_x[pl.ds(pl.multiple_of(i * cy, 8), cy), :] = (half_step * half_step) / permit
        return carry

    load_material.wait()
    lax.fori_loop(0, cx, coefs, 0, unroll=2)
    load.wait()
    for slot, member in enumerate(Y_MEMBERS):
        y_out[0, slot] = jnp.concatenate([grid_x[member, 1 + i, 0:1] for i in range(cx)], axis=0)
        y_out[1, slot] = jnp.concatenate([grid_x[member, 1 + i, cy - 1:cy] for i in range(cx)], axis=0)
    pl.semaphore_wait(barrier, count - 1)
    x_halo[0]()
    y_halo[0]()
    coef_plane = lambda i: coef_x[pl.ds(pl.multiple_of(i * cy, 8), cy), :]
    factor(cx, coef_plane, gain_x, pivot_x, left_x, right_x)
    line_x.mat_start(left_x, right_x)
    for j in range(cy):
        coef_y[j] = coef_x[pl.ds(j, cx, stride=cy), :]
    x_halo[1]()
    y_halo[1]()
    y_slot = {member: slot for slot, member in enumerate(Y_MEMBERS)}

    def forward_x(i, carry):
        centre = [grid_x[m, i + 1] for m in range(6)]
        slope_x = lambda m: 0.5 * (grid_x[m, i + 2] - grid_x[m, i])
        slope_y = lambda m: slope_rows(
            centre[m], y_low[y_slot[m], pl.ds(i, 1), :], y_high[y_slot[m], pl.ds(i, 1), :])
        right = updated(centre, slope_x, slope_y, coef_plane(i) * (1.0 / half_step), half_step)
        gain, pivot = gain_x[i], pivot_x[i]
        now = [right[m] * pivot + gain * carry[m] for m in range(6)]
        for m in range(6):
            solved_x[m, i] = now[m]
        return tuple(now)

    lax.fori_loop(0, cx, forward_x, (jnp.zeros((cy, cz), jnp.float32),) * 6, unroll=2)
    early = min(2, line_x.steps)
    line_x.mat_merge(0)
    sweep_back(cx, gain_x, solved_x)
    line_x.rhs_start(solved_x)
    if early > 1:
        line_x.mat_merge(1)
    factor(cy, lambda j: coef_y[j], gain_y, pivot_y, left_y, right_y)
    line_y.mat_start(left_y, right_y)
    for k in range(line_x.steps):
        if k >= early:
            line_x.mat_merge(k)
        for j in range(len(CHUNKS)):
            line_x.rhs_merge(k, j)
        if k < line_y.steps:
            line_y.mat_merge(k)
    for k in range(line_x.steps, line_y.steps):
        line_y.mat_merge(k)

    for i in range(cx):
        left, right = left_x[i], right_x[i]
        for m in range(6):
            grid_y[m, pl.ds(cx + i, cy, stride=cx), :] = (
                solved_x[m, i] + left * line_x.ends[0, m] + right * line_x.ends[1, m])
    mid_halo[0]()
    fill_weights(count, cx, cy, cz, cell_row, owner_row, weight_ref)
    mid_halo[1]()

    y_plane = lambda m, j: grid_y[m, pl.ds(pl.multiple_of(j * cx, 8), cx), :]

    def forward_y(j, carry):
        centre = [y_plane(m, j + 1) for m in range(6)]
        slope_y = lambda m: 0.5 * (y_plane(m, j + 2) - y_plane(m, j))
        slope_x = lambda m: slope_rows(
            centre[m], line_x.ends[0, m, pl.ds(j, 1), :], line_x.ends[1, m, pl.ds(j, 1), :])
        right = updated(centre, slope_x, slope_y, coef_y[j] * (1.0 / half_step), half_step)
        gain, pivot = gain_y[j], pivot_y[j]
        now = [right[m] * pivot + gain * carry[m] for m in range(6)]
        for m in range(6):
            solved_y[m, j] = now[m]
        return tuple(now)

    lax.fori_loop(0, cy, forward_y, (jnp.zeros((cx, cz), jnp.float32),) * 6, unroll=2)
    sweep_back(cy, gain_y, solved_y)
    line_y.rhs_start(solved_y)
    for k in range(line_y.steps):
        for j in range(len(CHUNKS)):
            line_y.rhs_merge(k, j)
    for j in range(cy):
        left, right = left_y[j], right_y[j]
        for m in range(6):
            value = solved_y[m, j] + left * line_y.ends[0, m] + right * line_y.ends[1, m]
            out_ref[m, pl.ds(j, cx, stride=cy), :] = value
            packed[pl.ds(j * 8 + m, cx, stride=cy * 8), :] = value

    save = pltpu.make_async_copy(out_ref, new_hbm, move_sems.at[1])
    save.start()
    patches = cell_smem.shape[0]

    def fetch(q, carry):
        for u in range(8):
            p = q * 8 + u
            line = cell_smem[p] // cz
            samples[pl.ds(p, 8, stride=patches), :] = packed[pl.ds(line * 8, 8), :]
        return carry

    lax.fori_loop(0, patches // 8, fetch, 0)
    spot = jnp.transpose(jnp.broadcast_to(cell_row[...] & (cz - 1), (cz, patches)))
    hit = lax.broadcasted_iota(jnp.int32, (patches, cz), 1) == spot
    column = lax.broadcasted_iota(jnp.int32, (patches, 128), 1)
    table = jnp.zeros((patches, 128), jnp.float32)
    for m in range(6):
        value = jnp.sum(jnp.where(hit, samples[pl.ds(m * patches, patches), :], 0.0), axis=1, keepdims=True)
        table = jnp.where(column == m, value, table)
    values = jnp.transpose(table)
    owner = owner_row[...]
    hot = (lax.broadcasted_iota(jnp.int32, (count, patches), 0) == owner).astype(jnp.float32)
    for m in range(6):
        spread[pl.ds(m * count, count), :] = hot * values[m:m + 1]
    product = lax.dot_general(spread[...], weight_ref[...], (((1,), (1,)), ((), ())),
                              precision=lax.Precision.HIGHEST, preferred_element_type=jnp.float32)
    angles = far_ref.shape[1]
    for m in range(6):
        for s in range(2):
            parts[pl.ds(s * 6 + m, count, stride=16), :] = (
                product[m * count:(m + 1) * count, s * angles:(s + 1) * angles])

    def piece(k):
        to = (me + k) % count
        return pltpu.make_async_remote_copy(
            parts.at[pl.ds(pl.multiple_of(to * 16, 16), 16)], landed.at[k],
            part_sems.at[0, k], part_sems.at[1, k],
            device_id=(to // ny, to % ny), device_id_type=MESH)

    def send(k, carry):
        piece(k).start()
        return carry

    lax.fori_loop(1, count, send, 0)
    for halo in (x_halo, y_halo, mid_halo):
        halo[2]()
    line_x.drain()
    line_y.drain()

    def add(k, total):
        piece(k).wait_recv()
        return total + landed[k]

    total = lax.fori_loop(1, count, add, parts[pl.ds(pl.multiple_of(me * 16, 16), 16), :])
    far_ref[...] = total[:12] * scale

    def done(k, carry):
        piece(k).wait_send()
        return carry

    lax.fori_loop(1, count, done, 0)
    save.wait()


def line_scratch(count, rows, lanes):
    steps = count.bit_length() - 1
    f32 = jnp.float32
    return [
        pltpu.VMEM((steps, 4, rows, lanes), f32),
        pltpu.VMEM((steps, 4, rows, lanes), f32),
        pltpu.VMEM((steps, 2, 6, rows, lanes), f32),
        pltpu.VMEM((steps, 2, 6, rows, lanes), f32),
        pltpu.VMEM((steps, 7, rows, lanes), f32),
        pltpu.VMEM((4, rows, lanes), f32),
        pltpu.VMEM((2, 6, rows, lanes), f32),
        pltpu.SemaphoreType.DMA((2, steps)),
        pltpu.SemaphoreType.DMA((2, steps, len(CHUNKS))),
    ]


def local(nx, ny, fields, material, permittivity, patch_cell, patch_owner):
    _, cx, cy, cz = fields.shape
    f32 = jnp.float32
    count = nx * ny
    patches = patch_cell.shape[0]
    vmem = pl.BlockSpec(memory_space=pltpu.VMEM)
    smem = pl.BlockSpec(memory_space=pltpu.SMEM)
    hbm = pl.BlockSpec(memory_space=pltpu.HBM)
    x_lines = [pltpu.VMEM((cx, cy, cz), f32)] * 4
    y_lines = [pltpu.VMEM((cy, cx, cz), f32)] * 4
    new_flat, far_field = pl.pallas_call(
        functools.partial(step_kernel, nx, ny, cx, cy, cz, 1.0 / math.sqrt(patches)),
        out_shape=(
            jax.ShapeDtypeStruct((6, cx * cy, cz), f32),
            jax.ShapeDtypeStruct((12, ANG_DEV), f32),
        ),
        in_specs=[hbm, hbm, smem, smem, vmem, vmem],
        out_specs=(hbm, vmem),
        scratch_shapes=[
            pltpu.VMEM((cx, cy, cz), jnp.int32),
            pltpu.VMEM((6, cx * cy, cz), f32),
            pltpu.VMEM((6, cx + 2, cy, cz), f32),
            pltpu.VMEM((6, (cy + 2) * cx, cz), f32),
            pltpu.VMEM((2, 4, cx, cz), f32),
            pltpu.VMEM((4, cx, cz), f32),
            pltpu.VMEM((4, cx, cz), f32),
            pltpu.VMEM((cx * cy, cz), f32),
            *x_lines,
            pltpu.VMEM((6, cx, cy, cz), f32),
            pltpu.VMEM((cy, cx, cz), f32),
            *y_lines,
            pltpu.VMEM((6, cy, cx, cz), f32),
            pltpu.VMEM((2 * ANG_DEV, patches), f32),
            pltpu.VMEM((cx * cy * 8, cz), f32),
            pltpu.VMEM((8 * patches, cz), f32),
            pltpu.VMEM((6 * count, patches), f32),
            pltpu.VMEM((count * 16, ANG_DEV), f32),
            pltpu.VMEM((count, 16, ANG_DEV), f32),
            pltpu.SemaphoreType.DMA,
            pltpu.SemaphoreType.DMA((2,)),
            pltpu.SemaphoreType.DMA((3, 4)),
            pltpu.SemaphoreType.DMA((2, count)),
            *line_scratch(nx, cy, cz),
            *line_scratch(ny, cx, cz),
        ],
        compiler_params=pltpu.CompilerParams(
            collective_id=0, has_side_effects=True),
        name="split_step",
    )(fields, material, permittivity, patch_cell, patch_cell[None, :], patch_owner.reshape(1, patches))
    return new_flat.reshape(fields.shape), far_field


def solution(mesh):
    return jax.shard_map(
        functools.partial(local, mesh.shape["gx"], mesh.shape["gy"]),
        mesh=mesh,
        in_specs=(
            P(None, "gx", "gy", None),
            P("gx", "gy", None),
            P(),
            P(("gx", "gy")),
            P(("gx", "gy"), None),
        ),
        out_specs=(P(None, "gx", "gy", None), P(None, ("gx", "gy"))),
        check_vma=False,
    )
```
